32 devices in a mesh: groups: 2 (over y), expert: 16 (over z, x, core).
Axes of the slice: x: 2, y: 2, z: 4, core: 2. Of those that a mesh axis runs over, the one named last changes fastest.
Arguments:
- tokens: bfloat16 [4096, 2048], P(('groups', 'expert')), parts along dimension 0, may hold values from -6 to 6
- route_ids: int32 [4096, 8], P(('groups', 'expert')), parts along dimension 0, may hold values from 0 to 15, all different within a row; in each aligned block of 128 rows (0 to 127, 128 to 255, ...) at most 80 rows name the same one
- gates: float32 [4096, 8], P(('groups', 'expert')), parts along dimension 0, may hold values from 0.3 to 1
- w_gate: bfloat16 [16, 2048, 768], P('expert'), may hold values from -0.125 to 0.125
- w_up: bfloat16 [16, 2048, 768], P('expert'), may hold values from -0.125 to 0.125
- w_down: bfloat16 [16, 768, 2048], P('expert'), may hold values from -0.21875 to 0.21875
Outputs:
- combined: bfloat16 [4096, 2048], P(('groups', 'expert')), parts along dimension 0
The draws below stay inside these ranges and needn't reach their ends.
There are 2 independent parts, one for each index of `groups`. The reference program is written for one: setup_inputs(seed, part) draws one part's arguments, and reference() takes and returns one part's arrays. A program takes and returns all parts, laid end to end along the dimension named above; an argument that names none is the same for every part. Nothing has to cross between parts.
Inputs may be any that keep to these rules, and one draw needn't show every extreme that they name: `route_ids`: each row names 8 different experts. In each aligned block of 128 rows (one device's tokens) no expert is named by more than 80 rows, a bound that some block reaches.
All inputs are finite; a program needn't handle non-finite values.
Results may differ from the reference program's by a relative error of at most 0.0058.
Values may be sent and summed in bfloat16 or wider, within the bound.
A program may use at most 128 MiB of HBM per device.

```python
import math
import jax
import jax.numpy as jnp
import numpy as np
from jax import lax

D = 2048
H = 768
TOP = 8
TOK_DEV = 128
EXPERTS = 16
TOKENS = 2048
SLOT = 80
N_EXPERT = 16


def level_of(stream_key, dims, shards, low, largest):
    gain = 1.0
    for position, parts in shards:
        draws = jax.random.uniform(jax.random.fold_in(jax.random.fold_in(stream_key, 6), position), (parts,), jnp.float32, low / len(shards), largest / len(shards))
        gain = gain * jnp.repeat(jnp.exp(draws), dims[position] // parts).reshape((-1,) + (1,) * (len(dims) - 1 - position))
    return gain


def shared_out(stream_key, own, number, rows, count, top, most, slope):
    sequence = jax.random.permutation(stream_key, count)
    crowded, ordinary = shares(count, rows * top, most, slope, True), shares(count, rows * top, most, slope, False)
    places = jnp.arange(count)

    def named(tallies, rotation):
        used = int((tallies > 0).sum())
        fixed = max(1, used // 4)
        moved = fixed + (places - fixed + rotation * (used - fixed)) % max(1, count - fixed)
        return jnp.zeros((count,), jnp.int32).at[sequence[jnp.where(places < fixed, places, moved)]].set(jnp.asarray(tallies, jnp.int32))

    tallies = jnp.where(number % 4 == 0, named(crowded, number // 4), named(ordinary, number - number // 4 - 1))
    mixed = jax.random.permutation(jax.random.fold_in(own, 3), count)
    source_of, receiver = mixed[0:count // 2 * 2:2], mixed[1:count // 2 * 2:2]
    room = jnp.minimum(tallies[source_of] - 1, most - tallies[receiver]) // 2
    room = jnp.where((source_of == sequence[0]) | (receiver == sequence[0]) | (tallies[receiver] == 0), 0, jnp.maximum(room, 0))
    moved = jax.random.randint(jax.random.fold_in(own, 4), (count // 2,), 0, 1 << 20) % (room + 1)
    tallies = tallies.at[source_of].add(-moved).at[receiver].add(moved)
    items = jnp.searchsorted(jnp.cumsum(tallies), jnp.arange(rows * top), side="right").astype(jnp.int32)
    table = items.reshape(top, rows).T
    table = table[jax.random.permutation(jax.random.fold_in(own, 1), rows)]
    rotation = jax.random.randint(jax.random.fold_in(own, 2), (rows, 1), 0, top)
    return jnp.take_along_axis(table, (jnp.arange(top)[None, :] + rotation) % top, axis=1)


def shares(amount, total, most, lean, full):
    portions = [(1 << 20) // math.isqrt(rank ** lean) + 1 for rank in range(1, amount + 1)]
    largest = most if full else min(most, max(-(-total // amount), total * portions[0] // sum(portions)))
    least = 1 if total - largest >= amount - 1 else 0
    holding, surplus = [largest] + [least] * (amount - 1), total - largest - least * (amount - 1)
    while surplus > 0:
        candidates = [i for i in range(1, amount) if holding[i] < largest] or [i for i in range(1, amount) if holding[i] < most]
        whole, budget = sum([portions[i] for i in candidates]), surplus
        for i in candidates:
            addition = min(most - holding[i], max(1, budget * portions[i] // whole), surplus)
            holding[i] = holding[i] + addition
            surplus = surplus - addition
    return np.array(holding)


def normal_values(rng, extent, spread, bound, cuts=(), held_as=jnp.bfloat16):
    array = jax.random.normal(rng, extent, jnp.float32) * spread
    if len(cuts) > 0:
        array = level_of(rng, extent, cuts, -0.22, 0.18) * array
    return jnp.clip(array, min=-bound, max=bound).astype(held_as)


def setup_inputs(seed: int = 0, part: int = 0) -> dict:
    key_list = jax.random.split(jax.random.key(seed), 7)
    own_keys = jax.random.split(jax.random.fold_in(key_list[6], part), 7)
    tokens = normal_values(own_keys[0], (TOKENS, D), 1.0, 6.0, ((0, 16),))
    route_ids_keys = jax.random.split(jax.random.fold_in(own_keys[1], 1), TOKENS // TOK_DEV)
    route_ids_turns = jax.random.permutation(jax.random.fold_in(own_keys[1], 3), TOKENS // TOK_DEV)
    route_ids = jax.vmap(lambda own, number: shared_out(jax.random.fold_in(own_keys[1], 2), own, number, TOK_DEV, EXPERTS, TOP, SLOT, 2))(route_ids_keys, route_ids_turns).reshape((TOKENS, TOP))
    gates = jnp.clip(0.3 + 0.7 * jax.random.uniform(own_keys[2], (TOKENS, TOP), jnp.float32) ** level_of(own_keys[2], (TOKENS, TOP), ((0, 16),), -0.2, 0.2), 0.3, 1.0)
    w_gate = normal_values(key_list[3], (EXPERTS, D, H), D ** -0.5, 0.125, ((0, 16),))
    w_up = normal_values(key_list[4], (EXPERTS, D, H), D ** -0.5, 0.125, ((0, 16),))
    w_down = normal_values(key_list[5], (EXPERTS, H, D), H ** -0.5, 0.21875, ((0, 16),))
    return {"tokens": tokens, "route_ids": route_ids, "gates": gates, "w_gate": w_gate, "w_up": w_up, "w_down": w_down}


def reference(tokens, route_ids, gates, w_gate, w_up, w_down):
    capacity = N_EXPERT * SLOT
    chosen = route_ids.reshape(-1)
    gate_list = gates.reshape(-1)

    def per_expert(summed, expert_id):
        match = chosen == expert_id
        chosen_rows = jnp.nonzero(match, size=capacity, fill_value=0)[0].astype(jnp.int32)
        live_mask = (jnp.arange(capacity).astype(jnp.int32) < jnp.sum(match.astype(jnp.int32))).astype(jnp.float32)
        token_rows = chosen_rows // TOP
        gathered = tokens[token_rows]
        gate_part = jnp.dot(gathered, w_gate[expert_id], preferred_element_type=jnp.float32)
        up_part = jnp.dot(gathered, w_up[expert_id], preferred_element_type=jnp.float32)
        hidden = (jax.nn.silu(gate_part) * up_part).astype(jnp.bfloat16)
        output = jnp.dot(hidden, w_down[expert_id], preferred_element_type=jnp.float32).astype(jnp.bfloat16)
        weight = gate_list[chosen_rows] * live_mask
        summed = summed.at[token_rows].add(output.astype(jnp.float32) * weight[:, None])
        return summed, None

    start = jnp.zeros((tokens.shape[0], tokens.shape[1]), jnp.float32)
    summed, _ = lax.scan(per_expert, start, jnp.arange(EXPERTS).astype(jnp.int32))
    return summed.astype(jnp.bfloat16)
```

```python
import jax
import jax.numpy as jnp
from jax import lax
from jax.sharding import PartitionSpec as P


def expert_mlp(block_data, gate_local, up_local, down_local):
    gate_part = jnp.dot(block_data, gate_local, preferred_element_type=jnp.float32)
    up_part = jnp.dot(block_data, up_local, preferred_element_type=jnp.float32)
    hidden = (jax.nn.silu(gate_part) * up_part).astype(jnp.bfloat16)
    return jnp.dot(hidden, down_local, preferred_element_type=jnp.float32)


def dense_on_device(tokens, route_ids, gates, w_gate, w_up, w_down):
    n_peers = lax.axis_size("expert")
    me = lax.axis_index("expert")
    experts = jnp.arange(n_peers, dtype=jnp.int32)
    weight = jnp.sum(
        jnp.where(route_ids[:, None, :] == experts[None, :, None], gates[:, None, :], 0.0), axis=2
    )
    weights = lax.all_gather(weight, "expert", axis=0, tiled=True)
    mine = lax.dynamic_slice_in_dim(weights, me, 1, axis=1)
    everyone = lax.all_gather(tokens, "expert", axis=0, tiled=True)
    part = expert_mlp(everyone, w_gate[0], w_up[0], w_down[0])
    part = part.astype(jnp.bfloat16).astype(jnp.float32) * mine
    return lax.psum_scatter(part.astype(jnp.bfloat16), "expert", scatter_dimension=0, tiled=True)


def routed_on_device(tokens, route_ids, gates, w_gate, w_up, w_down):
    n_peers = lax.axis_size("expert")
    tok_rows, top_k = route_ids.shape
    model_width = tokens.shape[1]
    capacity = 5 * tok_rows * top_k // (4 * n_peers)
    buffer_rows = n_peers * capacity
    assigned = tok_rows * top_k
    chosen = route_ids.reshape(-1)
    onehot = (chosen[:, None] == jnp.arange(n_peers, dtype=jnp.int32)[None, :]).astype(jnp.int32)
    running = jnp.cumsum(onehot, axis=0)
    position = jnp.sum(running * onehot, axis=1) - 1
    slot_of = chosen * capacity + position
    ordinal = jnp.arange(assigned, dtype=jnp.int32)
    anchor = jnp.zeros((buffer_rows,), jnp.int32).at[slot_of].set(ordinal)
    outgoing = tokens[anchor // top_k].reshape(n_peers, capacity, model_width)
    incoming = lax.all_to_all(outgoing, "expert", split_axis=0, concat_axis=0, tiled=True)
    n_src, n_items, _ = incoming.shape
    computed = expert_mlp(
        incoming.reshape(n_src * n_items, model_width), w_gate[0], w_up[0], w_down[0]
    ).astype(jnp.bfloat16)
    computed = computed.reshape(n_src, n_items, model_width)
    returned_rows = lax.all_to_all(computed, "expert", split_axis=0, concat_axis=0, tiled=True)
    returned = returned_rows.reshape(buffer_rows, model_width)[slot_of].astype(jnp.float32)
    combined = jnp.sum(returned.reshape(tok_rows, top_k, model_width) * gates[:, :, None], axis=1)
    return combined.astype(jnp.bfloat16)


def solution(mesh):
    n_peers = mesh.shape["expert"]

    def on_device(tokens, route_ids, gates, w_gate, w_up, w_down):
        dense = n_peers <= 4 * route_ids.shape[1]
        body = dense_on_device if dense else routed_on_device
        return body(tokens, route_ids, gates, w_gate, w_up, w_down)

    in_specs = (
        P(("groups", "expert"), None),
        P(("groups", "expert"), None),
        P(("groups", "expert"), None),
        P("expert", None, None),
        P("expert", None, None),
        P("expert", None, None),
    )
    out_specs = P(("groups", "expert"), None)
    return jax.shard_map(
        on_device, mesh=mesh, in_specs=in_specs, out_specs=out_specs, check_vma=False
    )
```

```python
import functools

import jax
import jax.numpy as jnp
from jax import lax
from jax.experimental import pallas as pl
from jax.experimental.pallas import tpu as pltpu
from jax.sharding import PartitionSpec as P


def expert_mlp(block_data, gate_local, up_local, down_local):
    gate_part = jnp.dot(block_data, gate_local, preferred_element_type=jnp.float32)
    up_part = jnp.dot(block_data, up_local, preferred_element_type=jnp.float32)
    hidden = (jax.nn.silu(gate_part) * up_part).astype(jnp.bfloat16)
    return jnp.dot(hidden, down_local, preferred_element_type=jnp.float32)


MESH = pl.DeviceIdType.MESH


def layer_kernel(
    n, rows, tok_ref, weight_ref, wg_hbm, wu_hbm, wd_hbm, out_ref,
    wg, wu, wd, held, gain, own, to_mate, from_mate, to_side, from_side, to_line, from_line,
    load_sem, gain_send, gain_recv, tok_recv, up_send, down_send, side_send, mate_send,
    mate_part_send, mate_part_recv, side_part_send, side_part_recv, line_part_send, line_part_recv,
):
    length = n // 4
    me = lax.axis_index("expert")
    c = lax.rem(me, 2)
    x = lax.rem(me // 2, 2)
    z = me // 4

    def index(z_at, x_at, c_at):
        return (z_at * 2 + x_at) * 2 + c_at

    mate = index(z, x, 1 - c)
    side = index(z, 1 - x, c)
    above = index(lax.rem(z + 1, length), x, c)
    below = index(lax.rem(z + length - 1, length), x, c)
    has_above = z < length - 1
    has_below = z > 0

    def block(ref, at):
        return ref.at[pl.ds(pl.multiple_of(at * rows, rows), rows), :]

    def remote(src, dst, send, recv, to):
        return pltpu.make_async_remote_copy(
            src_ref=src, dst_ref=dst, send_sem=send, recv_sem=recv,
            device_id={"expert": to}, device_id_type=MESH,
        )

    def nearest(k):
        both = jnp.minimum(z, length - 1 - z)
        near = (k + 1) // 2
        near = jnp.where(lax.rem(k, 2) == 1, near, -near)
        far = jnp.where(2 * z < length - 1, k - both, both - k)
        return z + jnp.where(k <= 2 * both, near, far)

    loads = [
        pltpu.make_async_copy(tok_ref, block(held, me), load_sem.at[0]),
        pltpu.make_async_copy(weight_ref.at[me], gain.at[me], load_sem.at[1]),
        pltpu.make_async_copy(wg_hbm, wg, load_sem.at[2]),
        pltpu.make_async_copy(wu_hbm, wu, load_sem.at[3]),
        pltpu.make_async_copy(wd_hbm, wd, load_sem.at[4]),
    ]
    for load in loads:
        load.start()

    barrier = pltpu.get_barrier_semaphore()
    for step in range(1, n):
        pl.semaphore_signal(
            barrier, inc=1, device_id={"expert": lax.rem(me + step, n)}, device_id_type=MESH
        )
    pl.semaphore_wait(barrier, n - 1)

    def tok_up(at):
        s = index(at, x, c)
        return remote(block(held, s), block(held, s), up_send.at[at], tok_recv.at[s], above)

    def tok_down(at):
        s = index(at, x, c)
        return remote(block(held, s), block(held, s), down_send.at[at], tok_recv.at[s], below)

    def tok_side(at):
        s = index(at, x, c)
        return remote(block(held, s), block(held, s), side_send.at[at], tok_recv.at[s], side)

    def tok_mate(s):
        return remote(block(held, s), block(held, s), mate_send.at[s // 2], tok_recv.at[s], mate)

    def tok_wait(s):
        remote(block(held, s), block(held, s), mate_send.at[0], tok_recv.at[s], mate).wait_recv()

    def gain_copy(to):
        return remote(weight_ref.at[to], gain.at[me], gain_send.at[to], gain_recv.at[me], to)

    loads[0].wait()
    tok_mate(me).start()

    @pl.when(has_above)
    def _():
        tok_up(z).start()

    @pl.when(has_below)
    def _():
        tok_down(z).start()

    tok_side(z).start()
    for step in range(1, n):
        gain_copy(lax.rem(me + step, n)).start()
    for load in loads[1:]:
        load.wait()

    def mate_part(at):
        return remote(
            block(to_mate, at), block(from_mate, at), mate_part_send.at[at], mate_part_recv.at[at], mate
        )

    def side_part(at):
        return remote(
            block(to_side, at), block(from_side, at), side_part_send.at[at], side_part_recv.at[at], side
        )

    def column(at):
        return jnp.transpose(gain[at])[:, 0:1]

    def expert(z_at, x_at):
        node = z_at * 2 + x_at
        mine, other = node * 2 + c, node * 2 + 1 - c
        for at in (mine, other):
            @pl.when(at != me)
            def _():
                remote(weight_ref.at[0], gain.at[at], gain_send.at[0], gain_recv.at[at], mate).wait_recv()
        data = jnp.concatenate([block(held, mine)[...], block(held, other)[...]], axis=0)
        gate_part = jnp.dot(data, wg[...], preferred_element_type=jnp.float32)
        up_part = jnp.dot(data, wu[...], preferred_element_type=jnp.float32)
        hidden = (gate_part / (1.0 + jnp.exp(-gate_part)) * up_part).astype(jnp.bfloat16)
        own_gain, other_gain = column(mine), column(other)
        width = wd.shape[1] // 4
        for piece in range(4):
            cols = slice(piece * width, (piece + 1) * width)
            out = jnp.dot(hidden, wd[:, cols], preferred_element_type=jnp.float32)
            out = out.astype(jnp.bfloat16).astype(jnp.float32)
            block(own, node)[:, cols] = out[:rows] * own_gain
            block(to_mate, node)[:, cols] = (out[rows:] * other_gain).astype(jnp.bfloat16)
        mate_part(node).start()

    def across(z_at):
        node = z_at * 2 + 1 - x
        mate_part(node).wait_recv()
        block(to_side, z_at)[...] = (
            block(own, node)[...] + block(from_mate, node)[...].astype(jnp.float32)
        ).astype(jnp.bfloat16)
        side_part(z_at).start()

    def step(t, carry):
        odd = lax.rem(t, 2)
        k = (t + 1) // 2

        @pl.when((odd == 1) & (k < length))
        def _():
            at = nearest(k)
            s = index(at, x, c)
            tok_wait(s)

            @pl.when((at < z) & has_above)
            def _():
                tok_up(at).start()

            @pl.when((at > z) & has_below)
            def _():
                tok_down(at).start()

            tok_side(at).start()
            tok_mate(s).start()

        x_at = lax.rem(x + odd, 2)
        z_at = nearest(k - odd)

        @pl.when(odd == 1)
        def _():
            s = index(z_at, 1 - x, c)
            tok_wait(s)
            tok_mate(s).start()

        tok_wait(index(z_at, x_at, 1 - c))
        expert(z_at, x_at)

        @pl.when((odd == 0) & (t > 0))
        def _():
            across(nearest(k - 1))

        return carry

    lax.fori_loop(0, 2 * length, step, 0)
    across(nearest(length - 1))

    def gathered(z_at):
        node = z_at * 2 + x
        mate_part(node).wait_recv()
        side_part(z_at).wait_recv()
        return (
            block(own, node)[...]
            + block(from_mate, node)[...].astype(jnp.float32)
            + block(from_side, z_at)[...].astype(jnp.float32)
        )

    def line_wait(slot):
        remote(
            block(to_line, 0), block(from_line, slot), line_part_send.at[0], line_part_recv.at[slot], mate
        ).wait_recv()

    def line_part(z_at, slot, to):
        return remote(
            block(to_line, z_at), block(from_line, slot), line_part_send.at[z_at], line_part_recv.at[slot], to
        )

    def relay(j, carry):
        low = length - 1 - z
        up_first = jnp.where(j < low, z + 1 + j, z - 1 - (j - low))
        down_first = jnp.where(j < z, z - 1 - j, z + 1 + (j - z))
        z_at = jnp.where(2 * z < length, up_first, down_first)
        is_up = z_at > z
        behind = (is_up & has_below) | ((z_at < z) & has_above)

        @pl.when(behind)
        def _():
            total = gathered(z_at)
            line_wait(z_at)
            block(to_line, z_at)[...] = (
                total + block(from_line, z_at)[...].astype(jnp.float32)
            ).astype(jnp.bfloat16)

        @pl.when(jnp.logical_not(behind))
        def _():
            block(to_line, z_at)[...] = gathered(z_at).astype(jnp.bfloat16)

        @pl.when(is_up)
        def _():
            line_part(z_at, z_at, above).start()

        @pl.when(z_at < z)
        def _():
            line_part(z_at, jnp.where(z_at == z - 1, length, z_at), below).start()

        return carry

    lax.fori_loop(0, length - 1, relay, 0)
    block(own, z * 2 + x)[...] = gathered(z)

    @pl.when(has_below)
    def _():
        line_wait(z)
        block(own, z * 2 + x)[...] += block(from_line, z)[...].astype(jnp.float32)

    @pl.when(has_above)
    def _():
        line_wait(length)
        block(own, z * 2 + x)[...] += block(from_line, length)[...].astype(jnp.float32)

    out_ref[...] = block(own, z * 2 + x)[...].astype(out_ref.dtype)

    def drain(at, carry):
        @pl.when((at <= z) & has_above)
        def _():
            tok_up(at).wait_send()

        @pl.when((at >= z) & has_below)
        def _():
            tok_down(at).wait_send()

        tok_side(at).wait_send()
        for x_at in range(2):
            tok_mate(index(at, x_at, c)).wait_send()
            mate_part(at * 2 + x_at).wait_send()
        side_part(at).wait_send()

        @pl.when(at != z)
        def _():
            line_part(at, at, mate).wait_send()

        return carry

    lax.fori_loop(0, length, drain, 0)
    for step_at in range(1, n):
        gain_copy(lax.rem(me + step_at, n)).wait_send()


def dense_on_device(tokens, route_ids, gates, w_gate, w_up, w_down):
    n = lax.axis_size("expert")
    rows, width = tokens.shape
    experts = jnp.arange(n, dtype=jnp.int32)
    weight = jnp.sum(
        jnp.where(route_ids.T[None, :, :] == experts[:, None, None], gates.T[None, :, :], 0.0), axis=1
    )
    weight = jnp.broadcast_to(weight[:, None, :], (n, 8, rows))
    nodes, length = n // 2, n // 4
    bf16, f32 = jnp.bfloat16, jnp.float32
    dma = pltpu.SemaphoreType.DMA
    vmem = pltpu.VMEM
    any_spec = pl.BlockSpec(memory_space=pl.ANY)
    vmem_spec = pl.BlockSpec(memory_space=pltpu.VMEM)
    return pl.pallas_call(
        functools.partial(layer_kernel, n, rows),
        out_shape=jax.ShapeDtypeStruct((rows, width), bf16),
        in_specs=[any_spec, vmem_spec, any_spec, any_spec, any_spec],
        out_specs=vmem_spec,
        scratch_shapes=[
            vmem(w_gate.shape[1:], bf16),
            vmem(w_up.shape[1:], bf16),
            vmem(w_down.shape[1:], bf16),
            vmem((n * rows, width), bf16),
            vmem((n, 8, rows), f32),
            vmem((nodes * rows, width), f32),
            vmem((nodes * rows, width), bf16),
            vmem((nodes * rows, width), bf16),
            vmem((length * rows, width), bf16),
            vmem((length * rows, width), bf16),
            vmem((length * rows, width), bf16),
            vmem(((length + 1) * rows, width), bf16),
            dma((5,)), dma((n,)), dma((n,)), dma((n,)),
            dma((length,)), dma((length,)), dma((length,)), dma((nodes,)),
            dma((nodes,)), dma((nodes,)), dma((length,)), dma((length,)), dma((length,)), dma((length + 1,)),
        ],
        compiler_params=pltpu.CompilerParams(
            collective_id=0, has_side_effects=True, vmem_limit_bytes=60 * 1024 * 1024
        ),
    )(tokens, weight, w_gate[0], w_up[0], w_down[0])


def routed_on_device(tokens, route_ids, gates, w_gate, w_up, w_down):
    n_peers = lax.axis_size("expert")
    tok_rows, top_k = route_ids.shape
    model_width = tokens.shape[1]
    capacity = 5 * tok_rows * top_k // (4 * n_peers)
    buffer_rows = n_peers * capacity
    assigned = tok_rows * top_k
    chosen = route_ids.reshape(-1)
    onehot = (chosen[:, None] == jnp.arange(n_peers, dtype=jnp.int32)[None, :]).astype(jnp.int32)
    running = jnp.cumsum(onehot, axis=0)
    position = jnp.sum(running * onehot, axis=1) - 1
    slot_of = chosen * capacity + position
    ordinal = jnp.arange(assigned, dtype=jnp.int32)
    anchor = jnp.zeros((buffer_rows,), jnp.int32).at[slot_of].set(ordinal)
    outgoing = tokens[anchor // top_k].reshape(n_peers, capacity, model_width)
    incoming = lax.all_to_all(outgoing, "expert", split_axis=0, concat_axis=0, tiled=True)
    n_src, n_items, _ = incoming.shape
    computed = expert_mlp(
        incoming.reshape(n_src * n_items, model_width), w_gate[0], w_up[0], w_down[0]
    ).astype(jnp.bfloat16)
    computed = computed.reshape(n_src, n_items, model_width)
    returned_rows = lax.all_to_all(computed, "expert", split_axis=0, concat_axis=0, tiled=True)
    returned = returned_rows.reshape(buffer_rows, model_width)[slot_of].astype(jnp.float32)
    combined = jnp.sum(returned.reshape(tok_rows, top_k, model_width) * gates[:, :, None], axis=1)
    return combined.astype(jnp.bfloat16)


def solution(mesh):
    n_peers = mesh.shape["expert"]

    def on_device(tokens, route_ids, gates, w_gate, w_up, w_down):
        dense = n_peers <= 4 * route_ids.shape[1]
        body = dense_on_device if dense else routed_on_device
        return body(tokens, route_ids, gates, w_gate, w_up, w_down)

    in_specs = (
        P(("groups", "expert"), None),
        P(("groups", "expert"), None),
        P(("groups", "expert"), None),
        P("expert", None, None),
        P("expert", None, None),
        P("expert", None, None),
    )
    out_specs = P(("groups", "expert"), None)
    return jax.shard_map(
        on_device, mesh=mesh, in_specs=in_specs, out_specs=out_specs, check_vma=False
    )
```

```python
import functools

import jax
import jax.numpy as jnp
from jax import lax
from jax.experimental import pallas as pl
from jax.experimental.pallas import tpu as pltpu
from jax.sharding import PartitionSpec as P


def expert_mlp(block_data, gate_local, up_local, down_local):
    gate_part = jnp.dot(block_data, gate_local, preferred_element_type=jnp.float32)
    up_part = jnp.dot(block_data, up_local, preferred_element_type=jnp.float32)
    hidden = (jax.nn.silu(gate_part) * up_part).astype(jnp.bfloat16)
    return jnp.dot(hidden, down_local, preferred_element_type=jnp.float32)


MESH = pl.DeviceIdType.MESH


def layer_kernel(
    n, rows, parts, group, crossing, late, tok_ref, weight_ref, wg_hbm, wu_hbm, wd_hbm, out_ref,
    wg, wu, wd, held, gain, spread, own, to_mate, from_mate, to_side, from_side, to_line, from_line,
    load_sem, gain_send, gain_recv, tok_recv, up_send, down_send, side_send, mate_send,
    mate_part_send, mate_part_recv, side_part_send, side_part_recv, line_part_send, line_part_recv,
):
    length = n // 4
    me = lax.axis_index("expert")
    c = lax.rem(me, 2)
    x = lax.rem(me // 2, 2)
    z = me // 4

    def index(z_at, x_at, c_at):
        return (z_at * 2 + x_at) * 2 + c_at

    mate = index(z, x, 1 - c)
    side = index(z, 1 - x, c)
    above = index(lax.rem(z + 1, length), x, c)
    below = index(lax.rem(z + length - 1, length), x, c)
    has_above = z < length - 1
    has_below = z > 0

    count = rows // parts

    def block(ref, at):
        return ref.at[pl.ds(pl.multiple_of(at * rows, rows), rows), :]

    def piece(ref, at, p):
        return ref.at[pl.ds(pl.multiple_of(at * rows + p * count, count), count), :]

    def one_of(p, chosen):
        found = p < 0
        for q in chosen:
            found = found | (p == q)
        return found

    def remote(src, dst, send, recv, to):
        return pltpu.make_async_remote_copy(
            src_ref=src, dst_ref=dst, send_sem=send, recv_sem=recv,
            device_id={"expert": to}, device_id_type=MESH,
        )

    def nearest(k):
        both = jnp.minimum(z, length - 1 - z)
        near = (k + 1) // 2
        near = jnp.where(lax.rem(k, 2) == 1, near, -near)
        far = jnp.where(2 * z < length - 1, k - both, both - k)
        return z + jnp.where(k <= 2 * both, near, far)

    loads = [
        pltpu.make_async_copy(tok_ref, block(held, me), load_sem.at[0]),
        pltpu.make_async_copy(weight_ref.at[me], gain.at[me], load_sem.at[1]),
        pltpu.make_async_copy(wg_hbm, wg, load_sem.at[2]),
        pltpu.make_async_copy(wu_hbm, wu, load_sem.at[3]),
        pltpu.make_async_copy(wd_hbm, wd, load_sem.at[4]),
    ]
    for load in loads:
        load.start()

    barrier = pltpu.get_barrier_semaphore()
    for step in range(1, n):
        pl.semaphore_signal(
            barrier, inc=1, device_id={"expert": lax.rem(me + step, n)}, device_id_type=MESH
        )
    pl.semaphore_wait(barrier, n - 1)

    def tok(p, s, sends, slot, to):
        return remote(piece(held, s, p), piece(held, s, p), sends.at[p, slot], tok_recv.at[p, s], to)

    def tok_up(p, s):
        return tok(p, s, up_send, s // 2, above)

    def tok_down(p, s):
        return tok(p, s, down_send, s // 2, below)

    def tok_side(p, s):
        return tok(p, s, side_send, s // 4, side)

    def tok_mate(p, s):
        return tok(p, s, mate_send, s // 2, mate)

    def tok_wait(p, s):
        tok_mate(p, s).wait_recv()

    def pass_on(p, s, at):
        @pl.when((at <= z) & has_above)
        def _():
            tok_up(p, s).start()

        @pl.when((at >= z) & has_below)
        def _():
            tok_down(p, s).start()

    def gain_copy(to):
        return remote(weight_ref.at[to], gain.at[me], gain_send.at[to], gain_recv.at[me], to)

    def mate_part(p, node):
        return remote(
            piece(to_mate, node, p), piece(from_mate, node, p),
            mate_part_send.at[p, node], mate_part_recv.at[p, node], mate,
        )

    def side_part(p, at):
        return remote(
            piece(to_side, at, p), piece(from_side, at, p),
            side_part_send.at[p, at], side_part_recv.at[p, at], side,
        )

    def line_part(p, node, slot, to):
        return remote(
            piece(to_line, node, p), piece(from_line, slot, p),
            line_part_send.at[p, node], line_part_recv.at[p, slot], to,
        )

    def own_column(p, k):
        at = nearest(k)
        s = index(at, x, c)

        @pl.when(k > 0)
        def _():
            tok_wait(p, s)

        pass_on(p, s, at)

        @pl.when((k == 0) | jnp.logical_not(one_of(p, crossing)))
        def _():
            tok_side(p, s).start()

        tok_mate(p, s).start()

    def other_column(p, k):
        at = nearest(k)
        s = index(at, 1 - x, c)
        tok_wait(p, s)

        @pl.when(one_of(p, crossing))
        def _():
            pass_on(p, s, at)

        tok_mate(p, s).start()

    def expert(p, k):
        @pl.when(lax.rem(k, group) == group - 1)
        def _():
            run_expert(p, [nearest(k - back) for back in reversed(range(group))])

    def run_expert(p, places):
        mine = [index(z_at, x_at, c) for z_at in places for x_at in (x, 1 - x)]
        others = [index(z_at, x_at, 1 - c) for z_at in places for x_at in (x, 1 - x)]
        for s in others:
            tok_wait(p, s)

        @pl.when(p == 0)
        def _():
            for s in mine + others:
                @pl.when(s != me)
                def _():
                    remote(weight_ref.at[0], gain.at[s], gain_send.at[0], gain_recv.at[s], mate).wait_recv()

                block(spread, s)[...] = jnp.broadcast_to(jnp.transpose(gain[s])[:, 0:1], (rows, 128))

        data = jnp.concatenate([piece(held, s, p)[...] for s in mine + others], axis=0)
        gate_part = jnp.dot(data, wg[...], preferred_element_type=jnp.float32)
        up_part = jnp.dot(data, wu[...], preferred_element_type=jnp.float32)
        hidden = (gate_part / (1.0 + jnp.exp(-gate_part)) * up_part).astype(jnp.bfloat16)
        scale = jnp.concatenate([piece(spread, s, p)[:, 0:1] for s in mine + others], axis=0)
        width = wd.shape[1] // 4
        for column in range(4):
            cols = slice(column * width, (column + 1) * width)
            out = jnp.dot(hidden, wd[:, cols], preferred_element_type=jnp.float32)
            out = out.astype(jnp.bfloat16).astype(jnp.float32) * scale
            for place, s in enumerate(mine):
                piece(own, s // 2, p)[:, cols] = out[place * count:(place + 1) * count]
            for place, s in enumerate(others):
                piece(to_mate, s // 2, p)[:, cols] = out[(len(mine) + place) * count:(len(mine) + place + 1) * count].astype(jnp.bfloat16)
        for s in others[::-1]:
            mate_part(p, s // 2).start()

    def across(p, k):
        z_at = nearest(k)
        for x_at in (1 - x, x):
            node = z_at * 2 + x_at
            mate_part(p, node).wait_recv()
            piece(own, node, p)[...] += piece(from_mate, node, p)[...].astype(jnp.float32)

        @pl.when(jnp.logical_not(one_of(p, late)))
        def _():
            piece(to_side, z_at, p)[...] = piece(own, z_at * 2 + 1 - x, p)[...].astype(jnp.bfloat16)
            side_part(p, z_at).start()

    def add_line(p, node, slot):
        line_part(p, 0, slot, mate).wait_recv()
        piece(own, node, p)[...] += piece(from_line, slot, p)[...].astype(jnp.float32)

    def add_side(p, z_at):
        side_part(p, z_at).wait_recv()
        piece(own, z_at * 2 + x, p)[...] += piece(from_side, z_at, p)[...].astype(jnp.float32)

    def relay_one(p, z_at, x_at, behind, slot, to):
        node = z_at * 2 + x_at

        @pl.when(behind)
        def _():
            add_line(p, node, node)

        piece(to_line, node, p)[...] = piece(own, node, p)[...].astype(jnp.bfloat16)
        line_part(p, node, slot, to).start()

    def relay_both(p, z_at, behind, step_to, to):
        def slot(x_at):
            landing = jnp.where((step_to < 0) & (z_at == z - 1), length, z_at)
            return landing * 2 + x_at

        @pl.when(one_of(p, late))
        def _():
            relay_one(p, z_at, 1 - x, behind, slot(1 - x), to)

        @pl.when(jnp.logical_not(one_of(p, late)))
        def _():
            add_side(p, z_at)

        relay_one(p, z_at, x, behind, slot(x), to)

    def relay(p, moment):
        up_at = moment - z
        down_at = 2 * length - 2 - z - moment

        @pl.when((up_at > z) & (up_at < length))
        def _():
            relay_both(p, up_at, has_below, 1, above)

        @pl.when((down_at < z) & (down_at >= 0))
        def _():
            relay_both(p, down_at, has_above, -1, below)

    def collect(p, x_at):
        @pl.when(has_below)
        def _():
            add_line(p, z * 2 + x_at, z * 2 + x_at)

        @pl.when(has_above)
        def _():
            add_line(p, z * 2 + x_at, length * 2 + x_at)

    def finish(p):
        @pl.when(one_of(p, late))
        def _():
            collect(p, 1 - x)
            piece(to_side, z, p)[...] = piece(own, z * 2 + 1 - x, p)[...].astype(jnp.bfloat16)
            side_part(p, z).start()

        collect(p, x)
        add_side(p, z)
        piece(out_ref, 0, p)[...] = piece(own, z * 2 + x, p)[...].astype(out_ref.dtype)

    def at_step(i, body):
        @pl.when((i >= 0) & (i < parts * length))
        def _():
            body(i // length, lax.rem(i, length))

    def returned(p, k):
        relay(p, k + 1)

    def returned_far(p, k):
        relay(p, k + 1 + length)

        @pl.when(k == length - 2)
        def _():
            finish(p)

    loads[0].wait()
    own_column(0, 0)
    for step in range(1, n):
        gain_copy(lax.rem(me + step, n)).start()
    for load in loads[1:]:
        load.wait()

    def step(i, carry):
        @pl.when(i > 0)
        def _():
            at_step(i, own_column)

        at_step(i - OTHER_LAG, other_column)
        at_step(i - EXPERT_LAG, expert)
        at_step(i - ACROSS_LAG, across)
        at_step(i - RETURN_LAG - length, returned_far)
        at_step(i - RETURN_LAG, returned)
        return carry

    lax.fori_loop(0, (parts + 1) * length + RETURN_LAG - 1, step, 0)

    def drain(i, carry):
        p, at = i // length, lax.rem(i, length)
        crosses, is_late = one_of(p, crossing), one_of(p, late)
        for x_at in range(2):
            s = index(at, x_at, c)
            here = x_at == x
            tok_mate(p, s).wait_send()

            @pl.when((at <= z) & has_above & (crosses | here))
            def _():
                tok_up(p, s).wait_send()

            @pl.when((at >= z) & has_below & (crosses | here))
            def _():
                tok_down(p, s).wait_send()

            mate_part(p, at * 2 + x_at).wait_send()

            @pl.when((at != z) & (is_late | here))
            def _():
                line_part(p, at * 2 + x_at, 0, mate).wait_send()

        @pl.when((at == z) | jnp.logical_not(crosses))
        def _():
            tok_side(p, index(at, x, c)).wait_send()

        @pl.when((at == z) | jnp.logical_not(is_late))
        def _():
            side_part(p, at).wait_send()

        return carry

    lax.fori_loop(0, parts * length, drain, 0)
    for step_at in range(1, n):
        gain_copy(lax.rem(me + step_at, n)).wait_send()


PARTS = 4
GROUP = 1
CROSSING = ()
LATE = ()
OTHER_LAG, EXPERT_LAG, ACROSS_LAG, RETURN_LAG = 1, 2, 3, 5


def dense_on_device(tokens, route_ids, gates, w_gate, w_up, w_down):
    n = lax.axis_size("expert")
    rows, width = tokens.shape
    experts = jnp.arange(n, dtype=jnp.int32)
    weight = jnp.sum(
        jnp.where(route_ids.T[None, :, :] == experts[:, None, None], gates.T[None, :, :], 0.0), axis=1
    )
    weight = jnp.broadcast_to(weight[:, None, :], (n, 8, rows))
    nodes, length = n // 2, n // 4
    bf16, f32 = jnp.bfloat16, jnp.float32
    dma = pltpu.SemaphoreType.DMA
    vmem = pltpu.VMEM
    any_spec = pl.BlockSpec(memory_space=pl.ANY)
    vmem_spec = pl.BlockSpec(memory_space=pltpu.VMEM)
    return pl.pallas_call(
        functools.partial(layer_kernel, n, rows, PARTS, GROUP, CROSSING, LATE),
        out_shape=jax.ShapeDtypeStruct((rows, width), bf16),
        in_specs=[any_spec, vmem_spec, any_spec, any_spec, any_spec],
        out_specs=vmem_spec,
        scratch_shapes=[
            vmem(w_gate.shape[1:], bf16),
            vmem(w_up.shape[1:], bf16),
            vmem(w_down.shape[1:], bf16),
            vmem((n * rows, width), bf16),
            vmem((n, 8, rows), f32),
            vmem((n * rows, 128), f32),
            vmem((nodes * rows, width), f32),
            vmem((nodes * rows, width), bf16),
            vmem((nodes * rows, width), bf16),
            vmem((length * rows, width), bf16),
            vmem((length * rows, width), bf16),
            vmem((nodes * rows, width), bf16),
            vmem(((nodes + 2) * rows, width), bf16),
            dma((5,)), dma((n,)), dma((n,)), dma((PARTS, n)),
            dma((PARTS, nodes)), dma((PARTS, nodes)), dma((PARTS, length)), dma((PARTS, nodes)),
            dma((PARTS, nodes)), dma((PARTS, nodes)), dma((PARTS, length)), dma((PARTS, length)),
            dma((PARTS, nodes)), dma((PARTS, nodes + 2)),
        ],
        compiler_params=pltpu.CompilerParams(
            collective_id=0, has_side_effects=True, vmem_limit_bytes=60 * 1024 * 1024
        ),
    )(tokens, weight, w_gate[0], w_up[0], w_down[0])


def routed_on_device(tokens, route_ids, gates, w_gate, w_up, w_down):
    n_peers = lax.axis_size("expert")
    tok_rows, top_k = route_ids.shape
    model_width = tokens.shape[1]
    capacity = 5 * tok_rows * top_k // (4 * n_peers)
    buffer_rows = n_peers * capacity
    assigned = tok_rows * top_k
    chosen = route_ids.reshape(-1)
    onehot = (chosen[:, None] == jnp.arange(n_peers, dtype=jnp.int32)[None, :]).astype(jnp.int32)
    running = jnp.cumsum(onehot, axis=0)
    position = jnp.sum(running * onehot, axis=1) - 1
    slot_of = chosen * capacity + position
    ordinal = jnp.arange(assigned, dtype=jnp.int32)
    anchor = jnp.zeros((buffer_rows,), jnp.int32).at[slot_of].set(ordinal)
    outgoing = tokens[anchor // top_k].reshape(n_peers, capacity, model_width)
    incoming = lax.all_to_all(outgoing, "expert", split_axis=0, concat_axis=0, tiled=True)
    n_src, n_items, _ = incoming.shape
    computed = expert_mlp(
        incoming.reshape(n_src * n_items, model_width), w_gate[0], w_up[0], w_down[0]
    ).astype(jnp.bfloat16)
    computed = computed.reshape(n_src, n_items, model_width)
    returned_rows = lax.all_to_all(computed, "expert", split_axis=0, concat_axis=0, tiled=True)
    returned = returned_rows.reshape(buffer_rows, model_width)[slot_of].astype(jnp.float32)
    combined = jnp.sum(returned.reshape(tok_rows, top_k, model_width) * gates[:, :, None], axis=1)
    return combined.astype(jnp.bfloat16)


def solution(mesh):
    n_peers = mesh.shape["expert"]

    def on_device(tokens, route_ids, gates, w_gate, w_up, w_down):
        dense = n_peers <= 4 * route_ids.shape[1]
        body = dense_on_device if dense else routed_on_device
        return body(tokens, route_ids, gates, w_gate, w_up, w_down)

    in_specs = (
        P(("groups", "expert"), None),
        P(("groups", "expert"), None),
        P(("groups", "expert"), None),
        P("expert", None, None),
        P("expert", None, None),
        P("expert", None, None),
    )
    out_specs = P(("groups", "expert"), None)
    return jax.shard_map(
        on_device, mesh=mesh, in_specs=in_specs, out_specs=out_specs, check_vma=False
    )
```
